512 devices in a mesh: node: 16 (over z, core), dev: 32 (over y, x).
Axes of the slice: x: 4, y: 8, z: 8, core: 2. Of those that a mesh axis runs over, the one named last changes fastest.
Arguments:
- amps: float32 [16, 32, 32, 1024], P('node', 'dev'), may hold values from -6 to 6
- amp_tile: int32 [16, 32], replicated, may hold values from 0 to 31, each once within a row
- ints: float32 [16, 32, 1024, 1024], P('node', 'dev'), may hold values from -0.1875 to 0.1875
- tasks: int32 [16, 256, 2], replicated, may hold values from 0 to 31, as said below
- pair_energy: float32 [16, 32], P('node', 'dev'), may hold values from -3 to -1
- virt_energy: float32 [16, 1024], replicated, may hold values from 0.5 to 3
Outputs:
- resid: float32 [16, 32, 16384], P('node', 'dev')
The draws below stay inside these ranges and needn't reach their ends.
Inputs may be any that keep to these rules, and one draw needn't show every extreme that they name: Each row amp_tile[n] is a permutation of the 32 contracted tile pairs. `tasks`: the first column names an output tile pair below 16, the second a contracted tile pair below 32; the (ab, cd) pairs of one pair block are distinct.
All inputs are finite; a program needn't handle non-finite values.
Results may differ from the reference program's by a relative error of at most 0.0003.
Values sent between devices are 32-bit elements; how exact they have to be, the bound alone decides.
A program may use at most 64 MiB of HBM per device.

```python
import jax
import jax.numpy as jnp
from jax import lax

TT = 1024
P_SIZE = 32
NVT = 32
NAB = 16
NIJ = 16
NTASK = 256


def draw_tasks(key, part):
    key_level, key_noise = jax.random.split(jax.random.fold_in(key, 7))
    level = jax.random.randint(key_level, (NIJ, NVT), 0, 4)
    noise = jax.random.randint(key_noise, (NIJ, NAB * NVT), 0, 2048)
    index = jnp.arange(NAB * NVT, dtype=jnp.int32)
    weight = jnp.take(level, index % NVT, axis=1)
    score = (noise + weight * 1024) * (NAB * NVT) + index[None, :]
    order = jnp.argsort(-score, axis=1)
    chosen = order[:, :NTASK]
    return jnp.stack([chosen // NVT, chosen % NVT], axis=-1).astype(jnp.int32)


def shard_levels(stream_key, dims, shards, least, high):
    def one(position, parts):
        steps = jax.random.uniform(jax.random.fold_in(jax.random.fold_in(stream_key, 6), position), (parts,), jnp.float32, least / len(shards), high / len(shards))
        return jnp.repeat(jnp.exp(steps), dims[position] // parts).reshape((-1,) + (1,) * (len(dims) - position - 1))

    level = one(*shards[0])
    for cut in shards[1:]:
        level = level * one(*cut)
    return level


def normal_values(rng, dims, deviation, reach, shards=(), kind=jnp.bfloat16):
    array = jax.random.normal(rng, dims, jnp.float32) * deviation
    if len(shards) > 0:
        array = shard_levels(rng, dims, shards, -0.22, 0.18) * array
    return jnp.clip(array, min=-reach, max=reach).astype(kind)


def setup_inputs(seed: int = 0) -> dict:
    streams_of = jax.random.split(jax.random.key(seed), 7)
    amps = normal_values(streams_of[0], (NIJ, NVT, P_SIZE, TT), 1.0, 6.0, ((0, 16), (1, 32)), jnp.float32)
    amp_tile = jax.vmap(lambda own: jax.random.permutation(own, NVT))(jax.random.split(streams_of[1], NIJ)).reshape((NIJ, NVT)).astype(jnp.int32)
    ints = normal_values(streams_of[2], (NAB, NVT, TT, TT), TT ** -0.5, 0.1875, ((0, 16), (1, 32)), jnp.float32)
    tasks = draw_tasks(jax.random.fold_in(streams_of[6], 71), 0)
    pair_energy = jnp.clip(-3.0 + 2.0 * jax.random.uniform(streams_of[4], (NIJ, P_SIZE), jnp.float32) ** shard_levels(streams_of[4], (NIJ, P_SIZE), ((0, 16), (1, 32)), -0.2, 0.2), -3.0, -1.0)
    virt_energy = jnp.clip(jax.random.uniform(streams_of[5], (NAB, TT), jnp.float32, 0.5, 3.0), 0.5, 3.0)
    return dict(amps=amps, amp_tile=amp_tile, ints=ints, tasks=tasks, pair_energy=pair_energy, virt_energy=virt_energy)


def tile_product(left, right):
    return lax.dot_general(left, right, (((1,), (1,)), ((), ())), precision=lax.Precision.HIGHEST, preferred_element_type=jnp.float32)


def reference(amps, amp_tile, ints, tasks, pair_energy, virt_energy):
    width = amps.shape[3]
    pairs = amps.shape[2]
    count = amps.shape[1]
    out_count = ints.shape[0]

    def row_work(block):
        slots = amp_tile[block]
        inverse = jnp.zeros((count,), jnp.int32).at[slots].set(jnp.arange(count, dtype=jnp.int32))
        ordered = amps[block][inverse]

        def task_step(ladder, task):
            ab_tile = task[0].astype(jnp.int32)
            cd_tile = task[1].astype(jnp.int32)
            product = tile_product(ordered[cd_tile], ints[ab_tile, cd_tile])
            offset = (ab_tile * width).astype(jnp.int32)
            current = lax.dynamic_slice_in_dim(ladder, offset, width, 1)
            return lax.dynamic_update_slice_in_dim(ladder, current + product, offset, 1), None

        ladder, _ = lax.scan(task_step, jnp.zeros((pairs, out_count * width), jnp.float32), tasks[block])
        return ladder

    ladder = lax.map(row_work, jnp.arange(amps.shape[0], dtype=jnp.int32))
    denominator = pair_energy[:, :, None] - virt_energy.reshape(1, 1, -1)
    return ladder / denominator
```

```python
import functools

import jax
import jax.numpy as jnp
from jax import lax
from jax.experimental import pallas as pl
from jax.experimental.pallas import tpu as pltpu
from jax.sharding import PartitionSpec as P

MESH = pl.DeviceIdType.MESH
NODES = 16
DEVS = 32
NX = 4
NY = 8
NZ = 8
PAIRS = 32
WIDTH = 1024
CHUNKS = ((0, 1), (7, 2), (6, 3), (5, 4))


def kernel(
    amps,
    slots,
    ints,
    tasks,
    out,
    x1,
    x2,
    inv,
    tiles,
    bf,
    bhi,
    blo,
    ahi,
    alo,
    part,
    from_left,
    from_right,
    r1,
    ry,
    r2,
    rz,
    v,
    local_sem,
    send_a,
    recv_a,
    send_c,
    recv_c,
    send_z,
    recv_up,
    recv_down,
    send_sib,
    recv_sib,
    send_x,
    recv_left,
    recv_right,
    send_y,
    recv_y,
    send_n,
    recv_n,
    send_f,
    recv_f,
):
    node = lax.axis_index("node")
    dev = lax.axis_index("dev")
    z, core = node // 2, node % 2
    y, x = dev // NX, dev % NX
    z_up = ((z + 1) % NZ) * 2 + core
    z_down = ((z + NZ - 1) % NZ) * 2 + core
    sibling = z * 2 + 1 - core
    x_right, x_left, x_far = (x + 1) % NX, (x + NX - 1) % NX, (x + 2) % NX

    def remote(src, dst, send, recv, node_id, dev_id):
        return pltpu.make_async_remote_copy(
            src_ref=src,
            dst_ref=dst,
            send_sem=send,
            recv_sem=recv,
            device_id=(node_id, dev_id),
            device_id_type=MESH,
        )

    def drain(ref, sem):
        pltpu.make_async_copy(ref, ref, sem).wait()

    load_b = pltpu.make_async_copy(ints.at[0, 0], bf, local_sem.at[0])
    load_b.start()

    barrier = pltpu.get_barrier_semaphore()

    @pl.loop(1, DEVS)
    def _(k):
        pl.semaphore_signal(barrier, inc=1, device_id=(node, (dev + k) % DEVS), device_id_type=MESH)

    @pl.loop(1, NODES)
    def _(k):
        pl.semaphore_signal(barrier, inc=1, device_id=((node + k) % NODES, dev), device_id_type=MESH)

    pl.semaphore_wait(barrier, DEVS + NODES - 2)

    def tile_of(ref, j):
        rows = pl.ds(pl.multiple_of((j // 8) * 8, 8), 8)
        columns = pl.ds(pl.multiple_of((j % 8) * 128, 128), 128)
        return ref.at[rows, columns]

    own_a = pltpu.make_async_copy(tile_of(amps.at[0, 0], dev), x1.at[dev], local_sem.at[1])
    own_a.start()

    @pl.loop(1, DEVS)
    def _(k):
        j = (dev + k) % DEVS
        remote(tile_of(amps.at[0, 0], j), x1.at[dev], send_a, recv_a, node, j).start()

    @pl.loop(0, DEVS)
    def _(c):
        found = jnp.int32(0)
        for s in range(DEVS):
            found = jnp.where(slots[node, s] == c, jnp.int32(s), found)
        inv[c] = found

    own_a.wait()
    drain(x1.at[pl.ds(0, DEVS - 1)], recv_a)

    own_tile = tiles.at[0, core]

    @pl.loop(1, DEVS)
    def _(k):
        c = (dev + k) % DEVS
        x2[c] = x1[inv[c]]
        remote(x2.at[c], tile_of(own_tile, dev), send_c, recv_c, node, c).start()

    x2[dev] = x1[inv[dev]]
    own_c = pltpu.make_async_copy(x2.at[dev], tile_of(own_tile, dev), local_sem.at[1])
    own_c.start()

    load_b.wait()

    @pl.loop(0, 16)
    def _(i):
        rows = pl.ds(pl.multiple_of(i * 64, 64), 64)
        whole = bf[rows, :]
        high = whole.astype(jnp.bfloat16)
        bhi[rows, :] = high
        blo[rows, :] = (whole - high.astype(jnp.float32)).astype(jnp.bfloat16)

    own_c.wait()
    drain(x1.at[pl.ds(0, DEVS - 1)], recv_c)

    def z_step(step):
        up, down = (NZ - step + 1) % NZ, step - 1
        rows_up = pl.ds(0, 16 if step == 4 else 32)
        rows_down = pl.ds(16, 16) if step == 4 else pl.ds(0, 32)
        remote(
            tiles.at[up, core, rows_up],
            tiles.at[NZ - step, core, rows_up],
            send_z,
            recv_up.at[step - 1],
            z_up,
            dev,
        ).start()
        remote(
            tiles.at[down, core, rows_down],
            tiles.at[step, core, rows_down],
            send_z,
            recv_down.at[step - 1],
            z_down,
            dev,
        ).start()

    def z_wait(step):
        rows_up = pl.ds(0, 16 if step == 4 else 32)
        rows_down = pl.ds(16, 16) if step == 4 else pl.ds(0, 32)
        drain(tiles.at[NZ - step, core, rows_up], recv_up.at[step - 1])
        drain(tiles.at[step, core, rows_down], recv_down.at[step - 1])

    def to_sibling(rel):
        remote(tiles.at[rel, core], tiles.at[rel, core], send_sib, recv_sib.at[rel], sibling, dev).start()

    def compute(q):
        for h, rel in enumerate(CHUNKS[q]):
            drain(tiles.at[rel, 1 - core], recv_sib.at[rel])
            for k in range(2):
                block = ((z + rel) % NZ) * 2 + k
                listed = tasks[block]
                hit = (listed[0:1, :] == node) & (listed[1:2, :] == dev)
                mask = jnp.max(hit.astype(jnp.float32), axis=1, keepdims=True)
                whole = tiles[rel, k] * mask
                high = whole.astype(jnp.bfloat16)
                rows = pl.ds((2 * h + k) * PAIRS, PAIRS)
                ahi[rows, :] = high
                alo[rows, :] = (whole - high.astype(jnp.float32)).astype(jnp.bfloat16)

        @pl.loop(0, 4)
        def _(i):
            columns = pl.ds(pl.multiple_of(i * 256, 256), 256)
            dims = (((1,), (1,)), ((), ()))
            dot = functools.partial(lax.dot_general, dimension_numbers=dims, preferred_element_type=jnp.float32)
            total = dot(ahi[...], blo[columns, :])
            total = total + dot(alo[...], bhi[columns, :])
            total = total + dot(ahi[...], bhi[columns, :])
            for h in range(2):
                for k in range(2):
                    for g in range(4):
                        start = (2 * h + k) * PAIRS + g * 8
                        part[q, g, h, k, :, columns] = total[start : start + 8, :]

    def send_dev(src, dst, recv, x_to):
        send = send_x.at[0 if x_to is x_right else 1]
        remote(src, dst, send, recv, node, y * NX + x_to).start()

    def x_first(q):
        send_dev(part.at[q, x_far, 0], from_left.at[q, 0], recv_left.at[q, 0], x_right)
        send_dev(part.at[q, x_far, 1], from_right.at[q, 0], recv_right.at[q, 0], x_left)
        send_dev(part.at[q, x_right, 1], from_left.at[q, 1], recv_left.at[q, 1], x_right)
        send_dev(part.at[q, x_left, 0], from_right.at[q, 1], recv_right.at[q, 1], x_left)

    def x_second(q):
        drain(from_left.at[q, 0], recv_left.at[q, 0])
        from_left[q, 0] = from_left[q, 0] + part[q, x_right, 0]
        send_dev(from_left.at[q, 0], from_left.at[q, 2], recv_left.at[q, 2], x_right)
        drain(from_right.at[q, 0], recv_right.at[q, 0])
        from_right[q, 0] = from_right[q, 0] + part[q, x_left, 1]
        send_dev(from_right.at[q, 0], from_right.at[q, 2], recv_right.at[q, 2], x_left)

    def x_last(q):
        for ref, sem in ((from_left, recv_left), (from_right, recv_right)):
            for i in (1, 2):
                drain(ref.at[q, i], sem.at[q, i])
        for h in range(2):
            total = part[q, x, h] + from_left[q, 2 - h] + from_right[q, 1 + h]
            for c in range(NY):
                r1[q, c, h] = total[:, :, c * 128 : (c + 1) * 128]
        ry[q, y] = r1[q, y]

        @pl.loop(1, NY)
        def _(k):
            to = (y + k) % NY
            remote(r1.at[q, to], ry.at[q, y], send_y, recv_y.at[q], node, to * NX + x).start()

    def y_last(q):
        drain(ry.at[q, pl.ds(0, NY - 1)], recv_y.at[q])
        total = ry[q, 0]
        for c in range(1, NY):
            total = total + ry[q, c]
        r2[q] = total
        for h, rel in enumerate(CHUNKS[q]):
            for k in range(2):
                to = ((z + rel) % NZ) * 2 + k
                if rel == 0:

                    @pl.when(to == node)
                    def _():
                        rz[node] = r2[q, h, k]

                    @pl.when(to != node)
                    def _():
                        remote(r2.at[q, h, k], rz.at[node], send_n, recv_n, to, dev).start()

                else:
                    remote(r2.at[q, h, k], rz.at[node], send_n, recv_n, to, dev).start()

    z_step(1)
    to_sibling(0)
    z_wait(1)
    z_step(2)
    to_sibling(1)
    to_sibling(7)
    compute(0)
    x_first(0)
    z_wait(2)
    z_step(3)
    to_sibling(2)
    to_sibling(6)
    compute(1)
    x_first(1)
    x_second(0)
    z_wait(3)
    z_step(4)
    to_sibling(3)
    to_sibling(5)
    compute(2)
    x_first(2)
    x_second(1)
    x_last(0)
    z_wait(4)
    to_sibling(4)
    compute(3)
    x_first(3)
    x_second(2)
    x_last(1)
    y_last(0)
    x_second(3)
    x_last(2)
    y_last(1)
    x_last(3)
    y_last(2)
    y_last(3)

    drain(rz.at[pl.ds(0, NODES - 1)], recv_n)
    mine = (y // 2) == x
    columns = pl.ds(pl.multiple_of(y * 128, 128), 128)
    for r in range(8):
        to = 8 * x + r
        v[r] = rz[:, r, :]

        @pl.when(to == dev)
        def _():
            out[:, columns] = rz[:, r, :]

        @pl.when(to != dev)
        def _():
            remote(v.at[r], out.at[:, columns], send_f, recv_f, node, to).start()

    @pl.when(mine)
    def _():
        drain(v.at[pl.ds(0, 7)], recv_f)
        drain(v.at[pl.ds(0, 7)], send_f)

    @pl.when(jnp.logical_not(mine))
    def _():
        drain(v, recv_f)
        drain(v, send_f)

    drain(x1.at[pl.ds(0, DEVS - 1)], send_a)
    drain(x2.at[pl.ds(0, DEVS - 1)], send_c)
    drain(tiles.at[pl.ds(0, 7), 0], send_z)
    drain(tiles.at[:, 0], send_sib)
    drain(from_left, send_x.at[0])
    drain(from_right, send_x.at[1])
    drain(r1.at[:, pl.ds(0, NY - 1)], send_y)
    drain(rz.at[pl.ds(0, NODES - 1)], send_n)


def exchange(amps, slots, ints, tasks):
    f32, bf16 = jnp.float32, jnp.bfloat16
    dma = pltpu.SemaphoreType.DMA
    hbm = pl.BlockSpec(memory_space=pl.ANY)
    vmem = pl.BlockSpec(memory_space=pltpu.VMEM)
    smem = pl.BlockSpec(memory_space=pltpu.SMEM)
    return pl.pallas_call(
        kernel,
        out_shape=jax.ShapeDtypeStruct((NODES, WIDTH), f32),
        in_specs=[hbm, smem, hbm, vmem],
        out_specs=vmem,
        scratch_shapes=[
            pltpu.VMEM((DEVS, 8, 128), f32),
            pltpu.VMEM((DEVS, 8, 128), f32),
            pltpu.SMEM((DEVS,), jnp.int32),
            pltpu.VMEM((NZ, 2, PAIRS, WIDTH), f32),
            pltpu.VMEM((WIDTH, WIDTH), f32),
            pltpu.VMEM((WIDTH, WIDTH), bf16),
            pltpu.VMEM((WIDTH, WIDTH), bf16),
            pltpu.VMEM((4 * PAIRS, WIDTH), bf16),
            pltpu.VMEM((4 * PAIRS, WIDTH), bf16),
            pltpu.VMEM((4, NX, 2, 2, 8, WIDTH), f32),
            pltpu.VMEM((4, 3, 2, 8, WIDTH), f32),
            pltpu.VMEM((4, 3, 2, 8, WIDTH), f32),
            pltpu.VMEM((4, NY, 2, 2, 8, 128), f32),
            pltpu.VMEM((4, NY, 2, 2, 8, 128), f32),
            pltpu.VMEM((4, 2, 2, 8, 128), f32),
            pltpu.VMEM((NODES, 8, 128), f32),
            pltpu.VMEM((8, NODES, 128), f32),
            dma((2,)),
            dma,
            dma,
            dma,
            dma,
            dma,
            dma((4,)),
            dma((4,)),
            dma,
            dma((NZ,)),
            dma((2,)),
            dma((4, 3)),
            dma((4, 3)),
            dma,
            dma((4,)),
            dma,
            dma,
            dma,
            dma,
        ],
        compiler_params=pltpu.CompilerParams(
            collective_id=0, has_side_effects=True, vmem_limit_bytes=48 * 1024 * 1024
        ),
    )(amps, slots, ints, tasks)


def on_device(amps, amp_tile, ints, tasks, pair_energy, virt_energy):
    ladder = exchange(amps, amp_tile, ints, jnp.transpose(tasks, (0, 2, 1)))
    return (ladder / (pair_energy[0, 0] - virt_energy)).reshape(1, 1, -1)


def solution(mesh):
    in_specs = (
        P("node", "dev", None, None),
        P(),
        P("node", "dev", None, None),
        P(),
        P("node", "dev"),
        P(),
    )
    return jax.shard_map(
        on_device, mesh=mesh, in_specs=in_specs, out_specs=P("node", "dev", None), check_vma=False
    )
```

```python
import jax
import jax.numpy as jnp
from jax import lax
from jax.experimental import pallas as pl
from jax.experimental.pallas import tpu as pltpu
from jax.sharding import PartitionSpec as P

MESH = pl.DeviceIdType.MESH
NODES = 16
DEVS = 32
NX = 4
NY = 8
NZ = 8
PAIRS = 32
WIDTH = 1024
CHUNKS = ((0,), (7, 1), (6, 2), (5, 3), (4,))
LAST = 4
PIECES = 16


def blocks(q):
    return 2 * len(CHUNKS[q])


def kernel(
    amps,
    slots,
    ints,
    tasks,
    pair_energy,
    virt_energy,
    out,
    x1,
    x2,
    slots_s,
    inv,
    tasks_v,
    energy_s,
    virt_v,
    masks,
    tiles,
    bf,
    bhi,
    blo,
    rows_f,
    rows_b,
    part,
    from_left,
    from_right,
    direct,
    r1,
    ry,
    r2,
    rz,
    sent_x,
    sent_y,
    local_sem,
    send_a,
    recv_a,
    send_c,
    recv_c,
    send_z,
    recv_z,
    send_sib,
    recv_sib,
    send_x,
    recv_left,
    recv_right,
    send_d,
    recv_d,
    send_y,
    recv_y,
    send_n,
    recv_n,
):
    node = lax.axis_index("node")
    dev = lax.axis_index("dev")
    z, core = node // 2, node % 2
    y, x = dev // NX, dev % NX
    sibling = z * 2 + 1 - core
    x_right, x_left, x_far = (x + 1) % NX, (x + NX - 1) % NX, (x + 2) % NX

    def remote(src, dst, send, recv, node_id, dev_id):
        return pltpu.make_async_remote_copy(
            src_ref=src,
            dst_ref=dst,
            send_sem=send,
            recv_sem=recv,
            device_id=(node_id, dev_id),
            device_id_type=MESH,
        )

    def drain(ref, sem):
        pltpu.make_async_copy(ref, ref, sem).wait()

    barrier = pltpu.get_barrier_semaphore()

    @pl.loop(1, DEVS)
    def _(k):
        pl.semaphore_signal(barrier, inc=1, device_id=(node, (dev + k) % DEVS), device_id_type=MESH)

    @pl.loop(1, NODES)
    def _(k):
        pl.semaphore_signal(barrier, inc=1, device_id=((node + k) % NODES, dev), device_id_type=MESH)

    loads = [
        pltpu.make_async_copy(slots, slots_s, local_sem.at[0]),
        pltpu.make_async_copy(tasks, tasks_v, local_sem.at[1]),
        pltpu.make_async_copy(pair_energy, energy_s, local_sem.at[2]),
        pltpu.make_async_copy(virt_energy, virt_v, local_sem.at[3]),
        pltpu.make_async_copy(ints.at[0, 0], bf, local_sem.at[4]),
    ]
    for load in loads:
        load.start()

    pl.semaphore_wait(barrier, DEVS + NODES - 2)

    relay = (dev % 2) == core

    def piece_of(j):
        rows = pl.ds(pl.multiple_of((j % 2) * 16, 16), 16)
        columns = pl.ds(pl.multiple_of((j // 2) * 128, 128), 128)
        return amps.at[0, 0, rows, columns]

    def send_piece(j):
        remote(piece_of(j), x1.at[dev], send_a, recv_a, node, 2 * j + core).start()

    @pl.loop(1, PIECES)
    def _(i):
        send_piece((dev // 2 + i) % PIECES)

    @pl.when(jnp.logical_not(relay))
    def _():
        send_piece(dev // 2)

    own_a = pltpu.make_async_copy(piece_of(dev // 2), x1.at[dev], local_sem.at[5])
    own_c = pltpu.make_async_copy(
        x2.at[dev],
        tiles.at[0, core, dev // 4, pl.ds(pl.multiple_of(((dev // 2) % 2) * 16, 16), 16)],
        local_sem.at[5],
    )

    @pl.when(relay)
    def _():
        own_a.start()

    loads[0].wait()

    @pl.loop(0, DEVS)
    def _(c):
        found = jnp.int32(0)
        for s in range(DEVS):
            found = jnp.where(slots_s[node, s] == c, jnp.int32(s), found)
        inv[c] = found

    @pl.when(relay)
    def _():
        own_a.wait()
        drain(x1.at[pl.ds(0, DEVS - 1)], recv_a)
        own_piece = tiles.at[0, core, dev // 4, pl.ds(pl.multiple_of(((dev // 2) % 2) * 16, 16), 16)]

        @pl.loop(1, DEVS)
        def _(k):
            c = (dev + k) % DEVS
            x2[c] = x1[inv[c]]
            remote(x2.at[c], own_piece, send_c, recv_c, node, c).start()

        x2[dev] = x1[inv[dev]]
        own_c.start()

    loads[4].wait()

    @pl.loop(0, 16)
    def _(i):
        rows = pl.ds(pl.multiple_of(i * 64, 64), 64)
        whole = bf[rows, :]
        high = whole.astype(jnp.bfloat16)
        bhi[rows, :] = high
        blo[rows, :] = (whole - high.astype(jnp.float32)).astype(jnp.bfloat16)

    loads[1].wait()

    @pl.loop(0, NODES)
    def _(i):
        listed = tasks_v[(2 * z + i) % NODES]
        hit = (listed[0:1, :] == node) & (listed[1:2, :] == dev)
        mask = jnp.max(hit.astype(jnp.float32), axis=1, keepdims=True)
        masks[i] = jnp.broadcast_to(mask, (1, 128))

    @pl.when(relay)
    def _():
        own_c.wait()
        drain(x1.at[pl.ds(0, PIECES - 1)], recv_c)

    @pl.when(jnp.logical_not(relay))
    def _():
        drain(x1.at[pl.ds(0, PIECES)], recv_c)

    def z_copy(src, dst, cut, sem, places):
        columns = pl.ds(4 * cut, 4) if cut is not None else pl.ds(0, 8)
        to = ((z + places) % NZ) * 2 + core
        return remote(tiles.at[src, core, columns], tiles.at[dst, core, columns], send_z, sem, to, dev)

    def z_start():
        z_copy(0, 7, None, recv_z.at[0], 1).start()
        z_copy(0, 1, None, recv_z.at[1], NZ - 1).start()
        for h in range(2):
            z_copy(0, 6, h, recv_z.at[2 + h], 2).start()
            z_copy(0, 2, 1 - h, recv_z.at[5 - h], NZ - 2).start()

    def z_near():
        drain(tiles.at[7, core], recv_z.at[0])
        to_sibling(7)
        drain(tiles.at[1, core], recv_z.at[1])
        to_sibling(1)

    def z_forward():
        for h in range(2):
            drain(tiles.at[6, core, pl.ds(4 * h, 4)], recv_z.at[2 + h])
            z_copy(6, 5, h, recv_z.at[6 + h], 1).start()
            if h == 0:
                z_copy(6, 4, 0, recv_z.at[10], 2).start()
            drain(tiles.at[2, core, pl.ds(4 * (1 - h), 4)], recv_z.at[5 - h])
            z_copy(2, 3, 1 - h, recv_z.at[9 - h], NZ - 1).start()
            if h == 0:
                z_copy(2, 4, 1, recv_z.at[11], NZ - 2).start()
        to_sibling(6)
        to_sibling(2)

    def z_far():
        for h in range(2):
            drain(tiles.at[5, core, pl.ds(4 * h, 4)], recv_z.at[6 + h])
            drain(tiles.at[3, core, pl.ds(4 * h, 4)], recv_z.at[8 + h])
        to_sibling(5)
        to_sibling(3)

    def z_opposite():
        for h in range(2):
            drain(tiles.at[4, core, pl.ds(4 * h, 4)], recv_z.at[10 + h])
        to_sibling(4)

    def to_sibling(rel):
        remote(tiles.at[rel, core], tiles.at[rel, core], send_sib, recv_sib.at[rel], sibling, dev).start()

    def compute(q):
        m = blocks(q)
        count = m * PAIRS
        for h, rel in enumerate(CHUNKS[q]):
            drain(tiles.at[rel, 1 - core], recv_sib.at[rel])
            for k in range(2):
                mask = masks[2 * rel + k]
                for g in range(NX):
                    rows_f[:, pl.ds(g * NY * m + 2 * h + k, NY, stride=m), :] = (
                        tiles[rel, k, :, pl.ds(g, NY, stride=NX), :] * mask
                    )
        for c in range(8):
            whole = rows_f[c, 0:count]
            high = whole.astype(jnp.bfloat16)
            rows_b[0:count, c * 128 : (c + 1) * 128] = high
            rows_b[count : 2 * count, c * 128 : (c + 1) * 128] = (whole - high.astype(jnp.float32)).astype(
                jnp.bfloat16
            )

        @pl.loop(0, 4)
        def _(i):
            columns = pl.ds(pl.multiple_of(i * 256, 256), 256)

            def dot(left, right):
                return lax.dot_general(
                    left, right, (((1,), (1,)), ((), ())), preferred_element_type=jnp.float32
                )

            both = dot(rows_b[0 : 2 * count, :], bhi[columns, :])
            low = dot(rows_b[0:count, :], blo[columns, :])
            total = both[0:count, :] + (both[count:, :] + low)
            for g in range(NX):
                for h in range(2):
                    start = (2 * g + h) * 4 * m
                    part[q, g, h, 0 : 4 * m, columns] = total[start : start + 4 * m, :]

    def send_dev(src, dst, side, recv, x_to):
        remote(src, dst, send_x.at[side], recv, node, y * NX + x_to).start()

    def x_first(q):
        rows = pl.ds(0, 4 * blocks(q))

        def own(g, h):
            return part.at[q, g, h, rows]

        if q == LAST:
            for d in (2, 1, 3):
                to = (x + d) % NX
                remote(
                    part.at[q, to, :, rows], direct.at[d - 1], send_d, recv_d.at[d - 1], node, y * NX + to
                ).start()
            return
        send_dev(own(x_far, 0), from_left.at[q, 0, rows], 0, recv_left.at[q, 0], x_right)
        send_dev(own(x_far, 1), from_right.at[q, 0, rows], 1, recv_right.at[q, 0], x_left)
        send_dev(own(x_right, 1), from_left.at[q, 1, rows], 0, recv_left.at[q, 1], x_right)
        send_dev(own(x_left, 0), from_right.at[q, 1, rows], 1, recv_right.at[q, 1], x_left)

    def x_second(q):
        n = 4 * blocks(q)
        rows = pl.ds(0, n)
        drain(from_left.at[q, 0, rows], recv_left.at[q, 0])
        from_left[q, 0, 0:n] = from_left[q, 0, 0:n] + part[q, x_right, 0, 0:n]
        send_dev(from_left.at[q, 0, rows], from_left.at[q, 2, rows], 0, recv_left.at[q, 2], x_right)
        drain(from_right.at[q, 0, rows], recv_right.at[q, 0])
        from_right[q, 0, 0:n] = from_right[q, 0, 0:n] + part[q, x_left, 1, 0:n]
        send_dev(from_right.at[q, 0, rows], from_right.at[q, 2, rows], 1, recv_right.at[q, 2], x_left)

    def x_last(q):
        m = blocks(q)
        n = 4 * m
        rows = pl.ds(0, n)
        if q == LAST:
            for d in range(3):
                drain(direct.at[d], recv_d.at[d])
        else:
            for ref, sem in ((from_left, recv_left), (from_right, recv_right)):
                for i in (1, 2):
                    drain(ref.at[q, i, rows], sem.at[q, i])
        for h in range(2):
            total = part[q, x, h, 0:n]
            if q == LAST:
                total = (total + direct[0, h]) + (direct[1, h] + direct[2, h])
            else:
                total = total + from_left[q, 2 - h, 0:n] + from_right[q, 1 + h, 0:n]
            r1[q, 4 * h : 4 * h + 4, 0:m] = total.reshape(4, m, 8, 128)
        ry[q, y, 0:m] = r1[q, y, 0:m]

        @pl.loop(1, NY)
        def _(k):
            to = (y + k) % NY
            remote(
                r1.at[q, to, pl.ds(0, m)], ry.at[q, y, pl.ds(0, m)], send_y, recv_y.at[q], node, to * NX + x
            ).start()

    def y_last(q):
        m = blocks(q)
        drain(ry.at[q, pl.ds(0, NY - 1), pl.ds(0, m)], recv_y.at[q])
        total = ry[q, 0, 0:m]
        for c in range(1, NY):
            total = total + ry[q, c, 0:m]
        r2[q, 0:m] = total
        for h, rel in enumerate(CHUNKS[q]):
            for k in range(2):
                to = ((z + rel) % NZ) * 2 + k
                src = r2.at[q, 2 * h + k]
                if rel == 0:

                    @pl.when(to == node)
                    def _():
                        rz[node] = r2[q, 2 * h + k]

                    @pl.when(to != node)
                    def _():
                        remote(src, rz.at[node], send_n, recv_n, to, dev).start()

                else:
                    remote(src, rz.at[node], send_n, recv_n, to, dev).start()

    z_start()
    to_sibling(0)
    compute(0)
    x_first(0)
    z_near()
    z_forward()
    compute(1)
    x_first(1)
    x_second(0)
    compute(2)
    x_first(2)
    x_second(1)
    z_far()
    z_opposite()
    x_last(0)
    compute(3)
    x_first(3)
    x_second(2)
    compute(4)
    x_first(4)
    x_second(3)
    x_last(1)
    y_last(0)
    x_last(2)
    y_last(1)
    x_last(3)
    y_last(2)
    loads[2].wait()
    loads[3].wait()
    virt = virt_v[...].reshape(NODES, 8, 128)
    x_last(4)
    y_last(3)
    y_last(4)

    drain(rz.at[pl.ds(0, NODES - 1)], recv_n)
    out[...] = rz[...] / (energy_s[0, 0] - virt)

    @pl.when(relay)
    def _():
        drain(x1.at[pl.ds(0, PIECES - 1)], send_a)
        drain(x2.at[pl.ds(0, DEVS - 1)], send_c)

    @pl.when(jnp.logical_not(relay))
    def _():
        drain(x1.at[pl.ds(0, PIECES)], send_a)

    drain(tiles.at[pl.ds(0, 7), 0], send_z)
    drain(tiles.at[:, 0], send_sib)
    drain(sent_x, send_x.at[0])
    drain(sent_x, send_x.at[1])
    drain(direct, send_d)
    drain(sent_y, send_y)
    drain(rz.at[pl.ds(0, NODES - 1)], send_n)


def exchange(*args):
    f32, bf16, i32 = jnp.float32, jnp.bfloat16, jnp.int32
    dma = pltpu.SemaphoreType.DMA
    return pl.pallas_call(
        kernel,
        out_shape=jax.ShapeDtypeStruct((NODES, 8, 128), f32),
        in_specs=[pl.BlockSpec(memory_space=pltpu.HBM)] * 6,
        out_specs=pl.BlockSpec(memory_space=pltpu.VMEM),
        scratch_shapes=[
            pltpu.VMEM((DEVS, 16, 128), f32),
            pltpu.VMEM((DEVS, 16, 128), f32),
            pltpu.SMEM((NODES, DEVS), i32),
            pltpu.SMEM((DEVS,), i32),
            pltpu.VMEM((NODES, 2, 256), i32),
            pltpu.SMEM((1, 1), f32),
            pltpu.VMEM((NODES, WIDTH), f32),
            pltpu.VMEM((NODES, 1, 128), f32),
            pltpu.VMEM((NZ, 2, 8, PAIRS, 128), f32),
            pltpu.VMEM((WIDTH, WIDTH), f32),
            pltpu.VMEM((WIDTH, WIDTH), bf16),
            pltpu.VMEM((WIDTH, WIDTH), bf16),
            pltpu.VMEM((8, 4 * PAIRS, 128), f32),
            pltpu.VMEM((8 * PAIRS, WIDTH), bf16),
            pltpu.VMEM((5, NX, 2, 16, WIDTH), f32),
            pltpu.VMEM((4, 3, 16, WIDTH), f32),
            pltpu.VMEM((4, 3, 16, WIDTH), f32),
            pltpu.VMEM((3, 2, 8, WIDTH), f32),
            pltpu.VMEM((5, NY, 4, 8, 128), f32),
            pltpu.VMEM((5, NY, 4, 8, 128), f32),
            pltpu.VMEM((5, 4, 8, 128), f32),
            pltpu.VMEM((NODES, 8, 128), f32),
            pltpu.VMEM((7, 3, 8, WIDTH), f32),
            pltpu.VMEM((8, NY - 1, 2, 8, 128), f32),
            dma((6,)),
            dma,
            dma,
            dma,
            dma,
            dma,
            dma((12,)),
            dma,
            dma((NZ,)),
            dma((2,)),
            dma((4, 3)),
            dma((4, 3)),
            dma,
            dma((3,)),
            dma,
            dma((5,)),
            dma,
            dma,
        ],
        compiler_params=pltpu.CompilerParams(
            collective_id=0, has_side_effects=True, vmem_limit_bytes=56 * 1024 * 1024
        ),
    )(*args)


def on_device(amps, amp_tile, ints, tasks, pair_energy, virt_energy):
    tasks = jnp.transpose(tasks, (0, 2, 1))
    return exchange(amps, amp_tile, ints, tasks, pair_energy, virt_energy).reshape(1, 1, -1)


def solution(mesh):
    in_specs = (
        P("node", "dev", None, None),
        P(),
        P("node", "dev", None, None),
        P(),
        P("node", "dev"),
        P(),
    )
    return jax.shard_map(
        on_device, mesh=mesh, in_specs=in_specs, out_specs=P("node", "dev", None), check_vma=False
    )
```

```python
import jax
import jax.numpy as jnp
from jax import lax
from jax.experimental import pallas as pl
from jax.experimental.pallas import tpu as pltpu
from jax.sharding import PartitionSpec as P

MESH = pl.DeviceIdType.MESH
NODES = 16
DEVS = 32
NX = 4
NY = 8
NZ = 8
PAIRS = 32
WIDTH = 1024
CHUNKS = ((0,), (7, 1), (6, 2), (5, 3), (4,))
DIRECT = (3, 4)
PIECES = 16


def blocks(q):
    return 2 * len(CHUNKS[q])


def kernel(
    amps,
    slots,
    ints,
    tasks,
    pair_energy,
    virt_energy,
    out,
    x1,
    x2,
    slots_s,
    inv,
    tasks_v,
    energy_s,
    virt_v,
    masks,
    tiles,
    bf,
    bhi,
    blo,
    rows_f,
    rows_b,
    part,
    from_left,
    from_right,
    direct,
    r1,
    ry,
    r2,
    rz,
    sent_x,
    sent_d,
    sent_y,
    local_sem,
    send_a,
    recv_a,
    send_c,
    recv_c,
    send_z,
    recv_z,
    send_sib,
    recv_sib,
    send_x,
    recv_left,
    recv_right,
    send_d,
    recv_d,
    send_y,
    recv_y,
    send_n,
    recv_n,
):
    node = lax.axis_index("node")
    dev = lax.axis_index("dev")
    z, core = node // 2, node % 2
    y, x = dev // NX, dev % NX
    sibling = z * 2 + 1 - core
    x_right, x_left, x_far = (x + 1) % NX, (x + NX - 1) % NX, (x + 2) % NX

    def remote(src, dst, send, recv, node_id, dev_id):
        return pltpu.make_async_remote_copy(
            src_ref=src,
            dst_ref=dst,
            send_sem=send,
            recv_sem=recv,
            device_id=(node_id, dev_id),
            device_id_type=MESH,
        )

    def drain(ref, sem):
        pltpu.make_async_copy(ref, ref, sem).wait()

    barrier = pltpu.get_barrier_semaphore()

    @pl.loop(1, DEVS)
    def _(k):
        pl.semaphore_signal(barrier, inc=1, device_id=(node, (dev + k) % DEVS), device_id_type=MESH)

    pl.semaphore_signal(barrier, inc=1, device_id=(sibling, dev), device_id_type=MESH)
    for d in (1, NZ - 1):
        pl.semaphore_signal(barrier, inc=1, device_id=(((z + d) % NZ) * 2 + core, dev), device_id_type=MESH)

    loads = [
        pltpu.make_async_copy(slots, slots_s, local_sem.at[0]),
        pltpu.make_async_copy(tasks, tasks_v, local_sem.at[1]),
        pltpu.make_async_copy(pair_energy, energy_s, local_sem.at[2]),
        pltpu.make_async_copy(virt_energy, virt_v, local_sem.at[3]),
        pltpu.make_async_copy(ints.at[0, 0], bf, local_sem.at[4]),
    ]
    for load in loads:
        load.start()

    pl.semaphore_wait(barrier, DEVS + 2)

    relay = (dev % 2) == core

    def piece_of(j):
        rows = pl.ds(pl.multiple_of((j % 2) * 16, 16), 16)
        columns = pl.ds(pl.multiple_of((j // 2) * 128, 128), 128)
        return amps.at[0, 0, rows, columns]

    def send_piece(j):
        remote(piece_of(j), x1.at[dev], send_a, recv_a, node, 2 * j + core).start()

    @pl.loop(1, PIECES)
    def _(i):
        send_piece((dev // 2 + i) % PIECES)

    @pl.when(jnp.logical_not(relay))
    def _():
        send_piece(dev // 2)

    own_a = pltpu.make_async_copy(piece_of(dev // 2), x1.at[dev], local_sem.at[5])
    own_c = pltpu.make_async_copy(
        x2.at[dev],
        tiles.at[0, core, dev // 4, pl.ds(pl.multiple_of(((dev // 2) % 2) * 16, 16), 16)],
        local_sem.at[5],
    )

    @pl.when(relay)
    def _():
        own_a.start()

    loads[0].wait()

    @pl.loop(0, DEVS)
    def _(c):
        found = jnp.int32(0)
        for s in range(DEVS):
            found = jnp.where(slots_s[node, s] == c, jnp.int32(s), found)
        inv[c] = found

    @pl.when(relay)
    def _():
        own_a.wait()
        drain(x1.at[pl.ds(0, DEVS - 1)], recv_a)
        own_piece = tiles.at[0, core, dev // 4, pl.ds(pl.multiple_of(((dev // 2) % 2) * 16, 16), 16)]

        @pl.loop(1, DEVS)
        def _(k):
            c = (dev + k) % DEVS
            x2[c] = x1[inv[c]]
            remote(x2.at[c], own_piece, send_c, recv_c, node, c).start()

        x2[dev] = x1[inv[dev]]
        own_c.start()

    loads[4].wait()

    @pl.loop(0, 16)
    def _(i):
        rows = pl.ds(pl.multiple_of(i * 64, 64), 64)
        whole = bf[rows, :]
        high = whole.astype(jnp.bfloat16)
        bhi[rows, :] = high
        blo[rows, :] = (whole - high.astype(jnp.float32)).astype(jnp.bfloat16)

    loads[1].wait()

    @pl.loop(0, NODES)
    def _(i):
        listed = tasks_v[(2 * z + i) % NODES]
        hit = (listed[0:1, :] == node) & (listed[1:2, :] == dev)
        mask = jnp.max(hit.astype(jnp.float32), axis=1, keepdims=True)
        masks[i] = jnp.broadcast_to(mask, (1, 128))

    @pl.when(relay)
    def _():
        own_c.wait()
        drain(x1.at[pl.ds(0, PIECES - 1)], recv_c)

    @pl.when(jnp.logical_not(relay))
    def _():
        drain(x1.at[pl.ds(0, PIECES)], recv_c)

    def z_copy(src, dst, half, sem, places):
        columns = pl.ds(4 * half, 4) if half is not None else pl.ds(0, 8)
        to = ((z + places) % NZ) * 2 + core
        return remote(tiles.at[src, core, columns], tiles.at[dst, core, columns], send_z, sem, to, dev)

    def z_send_up(step):
        z_copy((NZ - step + 1) % NZ, NZ - step, 0 if step == 4 else None, recv_z.at[2 * step - 2], 1).start()

    def z_send_down(step):
        z_copy(step - 1, step, 1 if step == 4 else None, recv_z.at[2 * step - 1], NZ - 1).start()

    def z_advance(step):
        if step == 4:
            for h in range(2):
                drain(tiles.at[4, core, pl.ds(4 * h, 4)], recv_z.at[6 + h])
            to_sibling(4)
            return
        drain(tiles.at[NZ - step, core], recv_z.at[2 * step - 2])
        z_send_up(step + 1)
        to_sibling(NZ - step)
        drain(tiles.at[step, core], recv_z.at[2 * step - 1])
        z_send_down(step + 1)
        to_sibling(step)

    def to_sibling(rel):
        remote(tiles.at[rel, core], tiles.at[rel, core], send_sib, recv_sib.at[rel], sibling, dev).start()

    def compute(q):
        m = blocks(q)
        count = m * PAIRS
        for h, rel in enumerate(CHUNKS[q]):
            drain(tiles.at[rel, 1 - core], recv_sib.at[rel])
            for k in range(2):
                mask = masks[2 * rel + k]
                for g in range(NX):
                    rows_f[:, pl.ds(g * NY * m + 2 * h + k, NY, stride=m), :] = (
                        tiles[rel, k, :, pl.ds(g, NY, stride=NX), :] * mask
                    )
        for c in range(8):
            whole = rows_f[c, 0:count]
            high = whole.astype(jnp.bfloat16)
            rows_b[0:count, c * 128 : (c + 1) * 128] = high
            rows_b[count : 2 * count, c * 128 : (c + 1) * 128] = (whole - high.astype(jnp.float32)).astype(
                jnp.bfloat16
            )

        @pl.loop(0, 4)
        def _(i):
            columns = pl.ds(pl.multiple_of(i * 256, 256), 256)

            def dot(left, right):
                return lax.dot_general(
                    left, right, (((1,), (1,)), ((), ())), preferred_element_type=jnp.float32
                )

            both = dot(rows_b[0 : 2 * count, :], bhi[columns, :])
            low = dot(rows_b[0:count, :], blo[columns, :])
            total = both[0:count, :] + (both[count:, :] + low)
            for g in range(NX):
                for h in range(2):
                    start = (2 * g + h) * 4 * m
                    part[q, g, h, 0 : 4 * m, columns] = total[start : start + 4 * m, :]

    def send_dev(src, dst, side, recv, x_to):
        remote(src, dst, send_x.at[side], recv, node, y * NX + x_to).start()

    def x_first(q):
        rows = pl.ds(0, 4 * blocks(q))

        def own(g, h):
            return part.at[q, g, h, rows]

        if q in DIRECT:
            i = DIRECT.index(q)
            for d in (2, 1, 3):
                to = (x + d) % NX
                remote(
                    part.at[q, to, :, rows],
                    direct.at[i, d - 1, :, rows],
                    send_d,
                    recv_d.at[i, d - 1],
                    node,
                    y * NX + to,
                ).start()
            return
        send_dev(own(x_far, 0), from_left.at[q, 0, rows], 0, recv_left.at[q, 0], x_right)
        send_dev(own(x_far, 1), from_right.at[q, 0, rows], 1, recv_right.at[q, 0], x_left)
        send_dev(own(x_right, 1), from_left.at[q, 1, rows], 0, recv_left.at[q, 1], x_right)
        send_dev(own(x_left, 0), from_right.at[q, 1, rows], 1, recv_right.at[q, 1], x_left)

    def x_second(q):
        n = 4 * blocks(q)
        rows = pl.ds(0, n)
        drain(from_left.at[q, 0, rows], recv_left.at[q, 0])
        from_left[q, 0, 0:n] = from_left[q, 0, 0:n] + part[q, x_right, 0, 0:n]
        send_dev(from_left.at[q, 0, rows], from_left.at[q, 2, rows], 0, recv_left.at[q, 2], x_right)
        drain(from_right.at[q, 0, rows], recv_right.at[q, 0])
        from_right[q, 0, 0:n] = from_right[q, 0, 0:n] + part[q, x_left, 1, 0:n]
        send_dev(from_right.at[q, 0, rows], from_right.at[q, 2, rows], 1, recv_right.at[q, 2], x_left)

    def x_last(q):
        m = blocks(q)
        n = 4 * m
        rows = pl.ds(0, n)
        if q in DIRECT:
            i = DIRECT.index(q)
            for d in range(3):
                drain(direct.at[i, d, :, rows], recv_d.at[i, d])
        else:
            for ref, sem in ((from_left, recv_left), (from_right, recv_right)):
                for i in (1, 2):
                    drain(ref.at[q, i, rows], sem.at[q, i])
        for h in range(2):
            total = part[q, x, h, 0:n]
            if q in DIRECT:
                total = (total + direct[i, 0, h, 0:n]) + (direct[i, 1, h, 0:n] + direct[i, 2, h, 0:n])
            else:
                total = total + from_left[q, 2 - h, 0:n] + from_right[q, 1 + h, 0:n]
            r1[q, 4 * h : 4 * h + 4, 0:m] = total.reshape(4, m, 8, 128)
        ry[q, y, 0:m] = r1[q, y, 0:m]

        @pl.loop(1, NY)
        def _(k):
            to = (y + k) % NY
            remote(
                r1.at[q, to, pl.ds(0, m)], ry.at[q, y, pl.ds(0, m)], send_y, recv_y.at[q], node, to * NX + x
            ).start()

    def y_last(q):
        m = blocks(q)
        drain(ry.at[q, pl.ds(0, NY - 1), pl.ds(0, m)], recv_y.at[q])
        total = ry[q, 0, 0:m]
        for c in range(1, NY):
            total = total + ry[q, c, 0:m]
        r2[q, 0:m] = total
        for h, rel in enumerate(CHUNKS[q]):
            for k in range(2):
                to = ((z + rel) % NZ) * 2 + k
                src = r2.at[q, 2 * h + k]
                if rel == 0:

                    @pl.when(to == node)
                    def _():
                        rz[node] = r2[q, 2 * h + k]

                    @pl.when(to != node)
                    def _():
                        remote(src, rz.at[node], send_n, recv_n, to, dev).start()

                else:
                    remote(src, rz.at[node], send_n, recv_n, to, dev).start()

    z_send_up(1)
    z_send_down(1)
    to_sibling(0)
    compute(0)
    x_first(0)
    z_advance(1)
    compute(1)
    x_first(1)
    x_second(0)
    z_advance(2)
    compute(2)
    x_first(2)
    x_second(1)
    x_last(0)
    z_advance(3)
    compute(3)
    x_first(3)
    x_second(2)
    x_last(1)
    y_last(0)
    z_advance(4)
    compute(4)
    x_first(4)
    x_last(2)
    y_last(1)
    x_last(3)
    y_last(2)
    loads[2].wait()
    loads[3].wait()
    virt = virt_v[...].reshape(NODES, 8, 128)
    x_last(4)
    y_last(3)
    y_last(4)

    drain(rz.at[pl.ds(0, NODES - 1)], recv_n)
    out[...] = rz[...] / (energy_s[0, 0] - virt)

    @pl.when(relay)
    def _():
        drain(x1.at[pl.ds(0, PIECES - 1)], send_a)
        drain(x2.at[pl.ds(0, DEVS - 1)], send_c)

    @pl.when(jnp.logical_not(relay))
    def _():
        drain(x1.at[pl.ds(0, PIECES)], send_a)

    drain(tiles.at[pl.ds(0, 7), 0], send_z)
    drain(tiles.at[:, 0], send_sib)
    drain(sent_x, send_x.at[0])
    drain(sent_x, send_x.at[1])
    drain(sent_d, send_d)
    drain(sent_y, send_y)
    drain(rz.at[pl.ds(0, NODES - 1)], send_n)


def exchange(*args):
    f32, bf16, i32 = jnp.float32, jnp.bfloat16, jnp.int32
    dma = pltpu.SemaphoreType.DMA
    return pl.pallas_call(
        kernel,
        out_shape=jax.ShapeDtypeStruct((NODES, 8, 128), f32),
        in_specs=[pl.BlockSpec(memory_space=pltpu.HBM)] * 6,
        out_specs=pl.BlockSpec(memory_space=pltpu.VMEM),
        scratch_shapes=[
            pltpu.VMEM((DEVS, 16, 128), f32),
            pltpu.VMEM((DEVS, 16, 128), f32),
            pltpu.SMEM((NODES, DEVS), i32),
            pltpu.SMEM((DEVS,), i32),
            pltpu.VMEM((NODES, 2, 256), i32),
            pltpu.SMEM((1, 1), f32),
            pltpu.VMEM((NODES, WIDTH), f32),
            pltpu.VMEM((NODES, 1, 128), f32),
            pltpu.VMEM((NZ, 2, 8, PAIRS, 128), f32),
            pltpu.VMEM((WIDTH, WIDTH), f32),
            pltpu.VMEM((WIDTH, WIDTH), bf16),
            pltpu.VMEM((WIDTH, WIDTH), bf16),
            pltpu.VMEM((8, 4 * PAIRS, 128), f32),
            pltpu.VMEM((8 * PAIRS, WIDTH), bf16),
            pltpu.VMEM((5, NX, 2, 16, WIDTH), f32),
            pltpu.VMEM((3, 3, 16, WIDTH), f32),
            pltpu.VMEM((3, 3, 16, WIDTH), f32),
            pltpu.VMEM((2, 3, 2, 16, WIDTH), f32),
            pltpu.VMEM((5, NY, 4, 8, 128), f32),
            pltpu.VMEM((5, NY, 4, 8, 128), f32),
            pltpu.VMEM((5, 4, 8, 128), f32),
            pltpu.VMEM((NODES, 8, 128), f32),
            pltpu.VMEM((5, 3, 8, WIDTH), f32),
            pltpu.VMEM((3, 6, 8, WIDTH), f32),
            pltpu.VMEM((8, NY - 1, 2, 8, 128), f32),
            dma((6,)),
            dma,
            dma,
            dma,
            dma,
            dma,
            dma((8,)),
            dma,
            dma((NZ,)),
            dma((2,)),
            dma((3, 3)),
            dma((3, 3)),
            dma,
            dma((2, 3)),
            dma,
            dma((5,)),
            dma,
            dma,
        ],
        compiler_params=pltpu.CompilerParams(
            collective_id=0, has_side_effects=True, vmem_limit_bytes=56 * 1024 * 1024
        ),
    )(*args)


def on_device(amps, amp_tile, ints, tasks, pair_energy, virt_energy):
    tasks = jnp.transpose(tasks, (0, 2, 1))
    return exchange(amps, amp_tile, ints, tasks, pair_energy, virt_energy).reshape(1, 1, -1)


def solution(mesh):
    in_specs = (
        P("node", "dev", None, None),
        P(),
        P("node", "dev", None, None),
        P(),
        P("node", "dev"),
        P(),
    )
    return jax.shard_map(
        on_device, mesh=mesh, in_specs=in_specs, out_specs=P("node", "dev", None), check_vma=False
    )
```
